32 devices in a mesh: group: 2 (over x), blk: 16 (over z, y, core).
Axes of the slice: x: 2, y: 2, z: 4, core: 2. Of those that a mesh axis runs over, the one named last changes fastest.
Arguments:
- head_rows: bfloat16 [16384, 512], P(('group', 'blk')), may hold values from -1.5 to 1.5
- tail_rows: bfloat16 [16384, 512], P(('group', 'blk')), may hold values from -1.5 to 1.5
- labels: int32 [3, 16384, 64], P(None, ('group', 'blk')), may hold values from 0 to 255
- relations: bfloat16 [2, 512, 512], replicated, may hold values from -0.0390625 to 0.0390625
- hot_ids: int32 [3], replicated, may hold values from 0 to 1
- row_order: int32 [1024], replicated, may hold values from 0 to 1023, each once
- master: float32 [1024, 512], P(('group', 'blk')), may hold values from -0.25 to 0.25
- grad_squares: float32 [1024, 512], P(('group', 'blk')), may hold values from 2516 to 251658
Outputs:
- new_master: float32 [1024, 512], P(('group', 'blk'))
- transformed: bfloat16 [16384, 512], P(('group', 'blk'))
The draws below stay inside these ranges and needn't reach their ends.
Inputs may be any that keep to these rules, and one draw needn't show every extreme that they name: `hot_ids`: relation ids of the cycle steps; they may repeat. A permutation: stored row j of master and grad_squares holds row row_order[j] of the relation table. Each word packs eight 0/1 labels, bit k for tail column 8 * w + k.
All inputs are finite; a program needn't handle non-finite values.
Results may differ from the reference program's by a relative error of at most 0.0062.
Values may be sent and summed in bfloat16 or wider, within the bound.
A program may use at most 64 MiB of HBM per device.

```python
import math
import jax
import jax.numpy as jnp
from jax import lax

D = 512
HEAD_DEV = 512
TAIL_DEV = 512
RELS = 2
STEPS = 3
HEADS = 16384
TAILS = 16384
N_GROUP = 2
N_BLK = 16


def set_ends(values, own_key, least, high):
    longest = values.shape.index(max(values.shape))
    spots = []
    for shift in (0, 1):
        where = [jax.random.randint(jax.random.fold_in(own_key, axis), (), 0, length) for axis, length in enumerate(values.shape)]
        where[longest] = (where[longest] + shift) % values.shape[longest]
        spots.append(tuple(where))
    return values.at[spots[0]].set(least).at[spots[1]].set(high)


def with_spikes(values, key, source, target, shards_of, factor):
    def block_of(axis_at):
        return (jnp.arange(values.shape[axis_at]) // (values.shape[axis_at] // shards_of)).reshape((-1,) + (1,) * (values.ndim - 1 - axis_at))

    near = jax.random.permutation(key, shards_of)[block_of(target)]
    second = (block_of(target) + shards_of // 2) % shards_of
    return jnp.where((block_of(source) == near) | (block_of(source) == second), factor * values, values)


def shard_levels(own_key, shape, split, low, largest):
    loudness, own = 1.0, jax.random.fold_in(own_key, 6)
    for axis_at, blocks in split:
        steps = jnp.exp(jax.random.uniform(jax.random.fold_in(own, axis_at), (blocks,), jnp.float32, low / len(split), largest / len(split)))
        loudness = loudness * jnp.repeat(steps, shape[axis_at] // blocks).reshape([-1 if axis == axis_at else 1 for axis in range(len(shape))])
    return loudness


def gaussian(stream_key, dims, width, bound, shards=(), kind=jnp.bfloat16):
    array = width * jax.random.normal(stream_key, dims, jnp.float32)
    if shards:
        array = array * shard_levels(stream_key, dims, shards, -0.22, 0.18)
    return jnp.clip(array, -bound, bound).astype(kind)


def gaussian_with(stream_key, shape, deviation, limit, cuts, heavy, kind=jnp.bfloat16):
    drawn = deviation * jax.random.normal(stream_key, shape, jnp.float32)
    if cuts:
        drawn = drawn * shard_levels(stream_key, shape, cuts, -0.22, 0.18)
    return jnp.clip(with_spikes(drawn, jax.random.fold_in(stream_key, 3), *heavy), -limit, limit).astype(kind)


def setup_inputs(seed: int = 0) -> dict:
    key_list = jax.random.split(jax.random.key(seed), 9)
    head_rows = gaussian_with(key_list[0], (HEADS, D), 0.25, 1.5, ((0, 32),), (0, 1, 32, 2.75))
    tail_rows = gaussian(key_list[1], (TAILS, D), 0.25, 1.5, ((0, 32),))
    labels = set_ends(jax.random.randint(key_list[2], (STEPS, HEADS, TAIL_DEV // 8), 0, 256), jax.random.fold_in(key_list[2], 1), 0, 255).astype(jnp.int32)
    relations = gaussian(key_list[3], (RELS, D, D), (HEADS * TAIL_DEV * STEPS // 1024) ** -0.5, 0.0390625)
    hot_ids = jax.random.randint(key_list[4], (STEPS,), 0, RELS).astype(jnp.int32)
    row_order = jax.random.permutation(key_list[5], RELS * D).astype(jnp.int32)
    master = gaussian(key_list[6], (RELS * D, D), D ** -0.5, 0.25, ((0, 32),), jnp.float32)
    grad_squares = jnp.clip(jnp.exp(math.log(251658.0) - 4.6054007 * jax.random.uniform(key_list[7], (RELS * D, D), jnp.float32) ** shard_levels(key_list[7], (RELS * D, D), ((0, 32),), -0.2, 0.2)), 2516.0, 251658.0)
    return dict(head_rows=head_rows, tail_rows=tail_rows, labels=labels, relations=relations, hot_ids=hot_ids, row_order=row_order, master=master, grad_squares=grad_squares)


learn_rate = 0.2
tiny_floor = 1e-10

def contract_rows(left, right):
    return lax.dot_general(left, right, (((0,), (0,)), ((), ())), preferred_element_type=jnp.float32)

def contract_cols(left, right):
    return lax.dot_general(left, right, (((1,), (1,)), ((), ())), preferred_element_type=jnp.float32)

def unpack_bits(words):
    shifts = jnp.arange(8, dtype=jnp.int32)
    bits = jnp.bitwise_and(jnp.right_shift(words[:, :, None], shifts[None, None, :]), 1)
    return bits.reshape(words.shape[0], words.shape[1] * 8)

def step_gradient(head_block, tail_block, label_words, operator):
    projected = contract_cols(operator, tail_block).astype(jnp.bfloat16)
    scores = jnp.dot(head_block, projected, preferred_element_type=jnp.float32)
    targets = unpack_bits(label_words).astype(jnp.float32)
    residual = (jax.nn.sigmoid(scores) - targets).astype(jnp.bfloat16)
    partial_sum = contract_rows(head_block, residual).astype(jnp.bfloat16)
    return jnp.dot(partial_sum, tail_block, preferred_element_type=jnp.float32)

def reference(head_rows, tail_rows, labels, relations, hot_ids, row_order, master, grad_squares):
    devices = N_GROUP * N_BLK

    def one_device(gradient, device):
        head_block = lax.dynamic_slice_in_dim(head_rows, device * HEAD_DEV, HEAD_DEV, 0)
        for cycle_step in range(STEPS):
            source = device // N_BLK * N_BLK + (device % N_BLK - cycle_step) % N_BLK
            tail_block = lax.dynamic_slice_in_dim(tail_rows, source * TAIL_DEV, TAIL_DEV, 0)
            label_block = lax.dynamic_slice_in_dim(labels[cycle_step], device * HEAD_DEV, HEAD_DEV, 0)
            relation_id = hot_ids[cycle_step]
            step_term = step_gradient(head_block, tail_block, label_block, relations[relation_id])
            gradient = gradient.at[relation_id].add(step_term)
        return (gradient, None)
    gradient, unused = lax.scan(one_device, jnp.zeros((RELS, D, D), jnp.float32), jnp.arange(devices, dtype=jnp.int32))
    table_rows = RELS * D
    stored = jnp.take(gradient.reshape(table_rows, D), row_order, axis=0)
    squares_new = grad_squares + stored * stored
    new_master = master - learn_rate * stored / (jnp.sqrt(squares_new) + tiny_floor)
    positions = jnp.zeros((table_rows,), jnp.int32).at[row_order].set(jnp.arange(table_rows, dtype=jnp.int32))
    chosen = lax.dynamic_slice_in_dim(positions, hot_ids[STEPS - 1] * D, D, 0)
    operator = jnp.take(new_master.astype(jnp.bfloat16), chosen, axis=0)
    transformed = jnp.dot(head_rows, operator, preferred_element_type=jnp.float32).astype(jnp.bfloat16)
    return (new_master, transformed)
```

```python
import functools

import jax
import jax.numpy as jnp
from jax import lax
from jax.experimental import pallas as pl
from jax.experimental.pallas import tpu as pltpu
from jax.sharding import PartitionSpec as P

learn_rate = 0.2
tiny_floor = 1e-10
CHUNKS = 4
PAIR = 2
PIECES = 2
SCHEDULE = [("b", 0), ("b", 2)] + [(stage, k) for stage in "gruG" for k in range(CHUNKS)] + [
    ("C", 0), ("C", 1), ("n", 0), ("C", 2), ("f", 0), ("C", 3), ("n", 2), ("f", 2),
]


def from_behind(block, axis, distance):
    devices = range(lax.axis_size(axis))
    route = [((i - distance) % len(devices), i) for i in devices]
    return lax.ppermute(block, axis, route)


def contract_rows(left, right):
    return lax.dot_general(
        left, right, (((0,), (0,)), ((), ())), preferred_element_type=jnp.float32
    )


def contract_cols(left, right):
    return lax.dot_general(
        left, right, (((1,), (1,)), ((), ())), preferred_element_type=jnp.float32
    )


def unpack_bits(words):
    shifts = jnp.arange(8, dtype=jnp.int32)
    bits = jnp.bitwise_and(jnp.right_shift(words[:, :, None], shifts[None, None, :]), 1)
    return bits.reshape(words.shape[0], words.shape[1] * 8)


def step_gradient(head_block, tail_block, label_words, operator):
    projected = contract_cols(operator, tail_block).astype(jnp.bfloat16)
    scores = jnp.dot(head_block, projected, preferred_element_type=jnp.float32)
    targets = unpack_bits(label_words).astype(jnp.float32)
    residual = (jax.nn.sigmoid(scores) - targets).astype(jnp.bfloat16)
    partial_sum = contract_rows(head_block, residual).astype(jnp.bfloat16)
    return jnp.dot(partial_sum, tail_block, preferred_element_type=jnp.float32)


def on_device(head_rows, tail_rows, labels, relations, hot_ids, row_order, master, grad_squares):
    rel_count = relations.shape[0]
    model_width = relations.shape[1]
    step_count = labels.shape[0]
    gradient = jnp.zeros((rel_count, model_width, model_width), jnp.float32)
    tail_block = tail_rows
    for cycle_step in range(step_count):
        if cycle_step > 0:
            tail_block = from_behind(tail_block, "blk", 1)
        relation_id = hot_ids[cycle_step]
        step_term = step_gradient(head_rows, tail_block, labels[cycle_step], relations[relation_id])
        gradient = gradient.at[relation_id].add(step_term)
    table_rows = rel_count * model_width
    flat_gradient = gradient.reshape(table_rows, model_width)
    groups = lax.axis_size("group")
    blocks = lax.axis_size("blk")
    slot_rows = row_order.reshape(groups, blocks, -1).transpose(1, 0, 2).reshape(-1)
    first_sum = lax.psum_scatter(
        jnp.take(flat_gradient, slot_rows, axis=0), "blk", scatter_dimension=0, tiled=True
    )
    owned_sum = lax.psum_scatter(first_sum, "group", scatter_dimension=0, tiled=True)
    squares_new = grad_squares + owned_sum * owned_sum
    new_master = master - learn_rate * owned_sum / (jnp.sqrt(squares_new) + tiny_floor)
    updated = new_master.astype(jnp.bfloat16)
    group_rows = lax.all_gather(updated, "group", axis=0, tiled=True)
    gathered = lax.all_gather(group_rows, "blk", axis=0, tiled=True)
    positions = (
        jnp.zeros((table_rows,), jnp.int32)
        .at[slot_rows]
        .set(jnp.arange(table_rows, dtype=jnp.int32))
    )
    chosen = lax.dynamic_slice_in_dim(
        positions, hot_ids[step_count - 1] * model_width, model_width, 0
    )
    operator = jnp.take(gathered, chosen, axis=0)
    transformed = jnp.dot(head_rows, operator, preferred_element_type=jnp.float32).astype(
        jnp.bfloat16
    )
    return (new_master, transformed)


MESH = pl.DeviceIdType.MESH


def fused_body(
    dims, hot_src, order_src, head_src, tail_src, labels_src, relations_src, master_src, squares_src,
    new_master, transformed,
    hot, order, head, tail, labels, relations, master, squares, tails, head_t, pick, near_pick, far_pick,
    picked, targets, partials, last_partial, gradient, stored_early, near_part, own, core_in, pair_sum, group_in,
    group_sum, rest_in, table, send_sems, recv_sems, tail_send, tail_recv, load_sems,
):
    groups, deep, rows, chunks, width = dims
    blocks = 4 * deep
    plane = 2 * groups
    step_count, model_width = labels.shape[0], head.shape[1]
    rel_count = relations.shape[0]
    total_rows = order.shape[1]
    g = lax.axis_index("group")
    b = lax.axis_index("blk")
    core = lax.rem(b, 2)
    mid = lax.rem(b // 2, 2)
    z = b // 4
    spot = g * 2 + mid
    partner = (g, b + 1 - 2 * core)
    plane_spots = [lax.rem(spot + d, plane) for d in range(1, plane)]
    group_peers = [(p // 2, z * 4 + lax.rem(p, 2) * 2 + core) for p in plane_spots]
    rest_peers = [(g, lax.rem(z + d, deep) * 4 + mid * 2 + core) for d in range(1, deep)]
    right = (g, lax.rem(b + 1, blocks))
    left = (g, lax.rem(b + blocks - 1, blocks))

    barrier = pltpu.get_barrier_semaphore()
    greeted = [partner] + group_peers + rest_peers + [right, left]
    for peer in greeted:
        pl.semaphore_signal(barrier, inc=1, device_id=peer, device_id_type=MESH)

    sources = (hot_src, head_src, relations_src, tail_src, labels_src, order_src, master_src, squares_src)
    filled = (hot, head, relations, tail, labels, order, master, squares)
    loads = [
        pltpu.make_async_copy(source, target, load_sems.at[i])
        for i, (source, target) in enumerate(zip(sources, filled))
    ]
    for load in loads:
        load.start()
    pl.semaphore_wait(barrier, len(greeted))

    def send(source, target, index, peer):
        copy = pltpu.make_async_remote_copy(
            src_ref=source, dst_ref=target, send_sem=send_sems.at[index],
            recv_sem=recv_sems.at[index], device_id=peer, device_id_type=MESH,
        )
        copy.start()
        return copy

    tail_count = tail.shape[0]
    piece = tail_count // PIECES
    pieces = [slice(p * piece, (p + 1) * piece) for p in range(PIECES)]

    def send_tail(step, p):
        source = tail_src if step == 0 else tails.at[step - 1]
        copy = pltpu.make_async_remote_copy(
            src_ref=source.at[pieces[p]], dst_ref=tails.at[step, pieces[p]],
            send_sem=tail_send.at[step, p], recv_sem=tail_recv.at[step, p],
            device_id=right, device_id_type=MESH,
        )
        copy.start()
        return copy

    def tail_of(step):
        return tail if step == 0 else tails.at[step - 1]

    f32, bf16 = jnp.float32, jnp.bfloat16
    word_count = labels.shape[1]
    last = step_count - 1
    hops = {(0, p): send_tail(0, p) for p in range(PIECES)}

    def arrive(step, p):
        hops[step - 1, p].wait_recv()
        if step < last:
            hops[step, p] = send_tail(step, p)

    def step_targets(step):
        lane = lax.broadcasted_iota(jnp.int32, (word_count, tail_count), 1)
        word = lax.broadcasted_iota(jnp.int32, (word_count, tail_count), 0)
        spread = (lane // 8 == word).astype(f32).astype(bf16)
        words = contract_rows(labels[step].astype(f32).astype(bf16), spread).astype(jnp.int32)
        bit = lax.broadcasted_iota(jnp.int32, words.shape, 1) % 8
        targets[step] = ((words >> bit) & 1).astype(f32).astype(bf16)

    def step_partial(step, span, heads):
        projected = contract_cols(relations[hot[step]], tail_of(step)[span]).astype(bf16)
        scores = jnp.dot(head[...], projected, preferred_element_type=f32)
        residual = (jax.nn.sigmoid(scores) - targets[step, :, span].astype(f32)).astype(bf16)
        return jnp.dot(heads, residual, preferred_element_type=f32).astype(bf16)

    def add_term(step):
        term = jnp.dot(partials[step], tail_of(step)[...], preferred_element_type=f32)
        for r in range(rel_count):
            share = (hot[step] == r).astype(f32) * term
            gradient[r] = share if step == 0 else gradient[r] + share

    def pick_rows():
        spread_order = jnp.broadcast_to(order[...].astype(f32), (128, total_rows)).T
        for j in range(0, total_rows, 128):
            ids = lax.broadcasted_iota(jnp.int32, (total_rows, 128), 1).astype(f32) + j
            pick[:, j : j + 128] = (spread_order == ids).astype(f32).astype(bf16)
        first = (hot[last] * model_width).astype(f32)
        chosen = jnp.concatenate([
            (spread_order - first == lax.broadcasted_iota(jnp.int32, (total_rows, 128), 1).astype(f32) + j)
            .astype(f32).astype(bf16)
            for j in range(0, model_width, 128)
        ], axis=1)
        picked[...] = jnp.dot(chosen, head_t[...], preferred_element_type=f32).astype(bf16).reshape(picked.shape)
        half = total_rows // 2
        near_pick[...] = picked[:, core].reshape(half, head.shape[0]).T
        far_pick[...] = picked[:, 1 - core].reshape(half, head.shape[0]).T

    for load in loads:
        load.wait()
    with jax.named_scope("s0"):
        head_t[...] = head[...].T
        step_targets(0)
        partials[0] = step_partial(0, slice(0, tail_count), head_t[...])
        add_term(0)
    with jax.named_scope("t12"):
        for step in range(1, step_count):
            step_targets(step)
    with jax.named_scope("a10"):
        if last > 1:
            arrive(1, 0)
    with jax.named_scope("pick"):
        pick_rows()
    for step in range(1, last):
        for p in range(PIECES):
            if step > 1 or p > 0:
                with jax.named_scope(f"a{step}{p}"):
                    arrive(step, p)
            with jax.named_scope(f"p{step}{p}"):
                partials[step, :, pieces[p]] = step_partial(step, pieces[p], head_t[...])
        with jax.named_scope(f"add{step}"):
            add_term(step)
    with jax.named_scope("stored"):
        stored_early[...] = jnp.dot(
            pick[...], gradient[...].reshape(total_rows, model_width).astype(bf16), preferred_element_type=f32
        )
    for p in range(PIECES):
        with jax.named_scope(f"a{last}{p}"):
            arrive(last, p)
        with jax.named_scope(f"p{last}{p}"):
            last_partial[:, pieces[p]] = step_partial(last, pieces[p], picked[...].reshape(total_rows, head.shape[0]))

    core_copies = [None] * chunks
    group_copies = [None] * chunks
    rest_copies = [None] * chunks
    back_rest = [None] * chunks
    back_group = [None] * chunks
    back_core = [None] * chunks

    def begin(k):
        cols = slice(k * width, (k + PAIR) * width)
        term = jnp.dot(last_partial[...], tail_of(last)[:, cols], preferred_element_type=f32)
        stored = (stored_early[:, cols] + term).astype(bf16)
        for i in range(k, k + PAIR):
            part = stored[:, (i - k) * width : (i - k + 1) * width]
            own[i] = part.reshape(groups, deep, 2, 2, rows, width)
            core_copies[i] = [send(own.at[i, :, :, :, 1 - core], core_in.at[i], (i, 0), partner)]

    def over_group(k):
        for copy in core_copies[k]:
            copy.wait_recv()
        pair_sum[k] = (own[k, :, :, :, core].astype(f32) + core_in[k].astype(f32)).astype(bf16)
        group_copies[k] = [
            send(pair_sum.at[k, p // 2, :, lax.rem(p, 2)], group_in.at[k, d], (k, 1 + d), peer)
            for d, (p, peer) in enumerate(zip(plane_spots, group_peers))
        ]

    def over_rest(k):
        for copy in group_copies[k]:
            copy.wait_recv()
        summed = own[k, g, :, mid, core].astype(f32) + core_in[k, g, :, mid].astype(f32)
        for d in range(plane - 1):
            summed = summed + group_in[k, d].astype(f32)
        group_sum[k] = summed.astype(bf16)
        rest_copies[k] = [
            send(
                group_sum.at[k, lax.rem(z + d + 1, deep)], rest_in.at[k, d],
                (k, plane + d), peer,
            )
            for d, peer in enumerate(rest_peers)
        ]

    def update(k):
        cols = slice(k * width, (k + 1) * width)
        for copy in rest_copies[k]:
            copy.wait_recv()
        summed = group_sum[k, z].astype(f32)
        for d in range(deep - 1):
            summed = summed + rest_in[k, d].astype(f32)
        squares_new = squares[:, cols] + summed * summed
        updated = master[:, cols] - learn_rate * summed / (jnp.sqrt(squares_new) + tiny_floor)
        new_master[:, cols] = updated
        table[k, g, z, mid, core] = updated.astype(bf16)
        mine = table.at[k, g, z, mid, core]
        back_rest[k] = [
            send(mine, mine, (k, plane + deep - 1 + d), peer)
            for d, peer in enumerate(rest_peers)
        ]

    def gather_group(k):
        for copy in back_rest[k]:
            copy.wait_recv()
        mine = table.at[k, g, :, mid, core]
        back_group[k] = [
            send(mine, mine, (k, plane + 2 * (deep - 1) + d), peer)
            for d, peer in enumerate(group_peers)
        ]

    def gather_core(k):
        for copy in back_group[k]:
            copy.wait_recv()
        mine = table.at[k, :, :, :, core]
        back_core[k] = [send(mine, mine, (k, 2 * (plane + deep - 2) + 1), partner)]

    def near(k):
        operator = jnp.concatenate(
            [table[i, :, :, :, core].reshape(total_rows // 2, width) for i in range(k, k + PAIR)], axis=1
        )
        near_part[k // PAIR] = jnp.dot(near_pick[...], operator, preferred_element_type=f32)

    def finish(k):
        cols = slice(k * width, (k + PAIR) * width)
        for i in range(k, k + PAIR):
            for copy in back_core[i]:
                copy.wait_recv()
        operator = jnp.concatenate(
            [table[i, :, :, :, 1 - core].reshape(total_rows // 2, width) for i in range(k, k + PAIR)], axis=1
        )
        far = jnp.dot(far_pick[...], operator, preferred_element_type=f32)
        transformed[:, cols] = (near_part[k // PAIR] + far).astype(bf16)

    stages = dict(
        b=begin, g=over_group, r=over_rest, u=update, G=gather_group, C=gather_core, n=near, f=finish
    )
    for stage, k in SCHEDULE:
        with jax.named_scope(f"{stage}{k}"):
            stages[stage](k)

    for copy in hops.values():
        copy.wait_send()
    for k in range(chunks):
        for lot in (core_copies, group_copies, rest_copies, back_rest, back_group, back_core):
            for copy in lot[k]:
                copy.wait_send()


def on_device_fused(head_rows, tail_rows, labels, relations, hot_ids, row_order, master, grad_squares):
    groups = lax.axis_size("group")
    deep = lax.axis_size("blk") // 4
    rows, model_width = master.shape
    steps = labels.shape[0]
    heads = head_rows.shape[0]
    table_rows = relations.shape[0] * model_width
    chunks = CHUNKS
    width = model_width // chunks
    order = row_order.reshape(1, -1)
    copies = 2 * (2 * groups + deep - 2) + 2
    bf16 = jnp.bfloat16
    vmem = pl.BlockSpec(memory_space=pltpu.VMEM)
    hbm = pl.BlockSpec(memory_space=pltpu.HBM)
    words = labels.transpose(0, 2, 1)
    results = pl.pallas_call(
        functools.partial(fused_body, (groups, deep, rows, chunks, width)),
        out_shape=(
            pltpu.VMEM(master.shape, jnp.float32),
            pltpu.VMEM((heads, model_width), bf16),
        ),
        in_specs=[hbm] * 8,
        out_specs=(vmem, vmem),
        scratch_shapes=[pltpu.SMEM(hot_ids.shape, hot_ids.dtype), pltpu.VMEM(order.shape, order.dtype)] + [
            pltpu.VMEM(x.shape, x.dtype)
            for x in (head_rows, tail_rows, words, relations, master, grad_squares)
        ] + [
            pltpu.VMEM((steps - 1,) + tail_rows.shape, bf16),
            pltpu.VMEM((model_width, heads), bf16),
            pltpu.VMEM((table_rows, table_rows), bf16),
            pltpu.VMEM((heads, table_rows // 2), bf16),
            pltpu.VMEM((heads, table_rows // 2), bf16),
            pltpu.VMEM((groups * deep * 2, 2, rows, heads), bf16),
            pltpu.VMEM((steps, heads, tail_rows.shape[0]), bf16),
            pltpu.VMEM((steps - 1, model_width, tail_rows.shape[0]), bf16),
            pltpu.VMEM((table_rows, tail_rows.shape[0]), bf16),
            pltpu.VMEM(relations.shape, jnp.float32),
            pltpu.VMEM((table_rows, model_width), jnp.float32),
            pltpu.VMEM((chunks // PAIR, heads, PAIR * width), jnp.float32),
            pltpu.VMEM((chunks, groups, deep, 2, 2, rows, width), bf16),
            pltpu.VMEM((chunks, groups, deep, 2, rows, width), bf16),
            pltpu.VMEM((chunks, groups, deep, 2, rows, width), bf16),
            pltpu.VMEM((chunks, 2 * groups - 1, deep, rows, width), bf16),
            pltpu.VMEM((chunks, deep, rows, width), bf16),
            pltpu.VMEM((chunks, deep - 1, rows, width), bf16),
            pltpu.VMEM((chunks, groups, deep, 2, 2, rows, width), bf16),
            pltpu.SemaphoreType.DMA((chunks, copies)),
            pltpu.SemaphoreType.DMA((chunks, copies)),
            pltpu.SemaphoreType.DMA((steps - 1, PIECES)),
            pltpu.SemaphoreType.DMA((steps - 1, PIECES)),
            pltpu.SemaphoreType.DMA((8,)),
        ],
        compiler_params=pltpu.CompilerParams(
            collective_id=0, has_side_effects=True, vmem_limit_bytes=60000 * 1024
        ),
        name="rescal_update",
    )(hot_ids, order, head_rows, tail_rows, words, relations, master, grad_squares)
    return keep_results(results)


def keep_body(first, second, first_out, second_out, sems):
    copies = [
        pltpu.make_async_copy(first, first_out, sems.at[0]),
        pltpu.make_async_copy(second, second_out, sems.at[1]),
    ]
    for copy in copies:
        copy.start()
    for copy in copies:
        copy.wait()


def keep_results(results):
    vmem = pl.BlockSpec(memory_space=pltpu.VMEM)
    hbm = pl.BlockSpec(memory_space=pltpu.HBM)
    return tuple(pl.pallas_call(
        keep_body,
        out_shape=tuple(jax.ShapeDtypeStruct(r.shape, r.dtype) for r in results),
        in_specs=[vmem, vmem],
        out_specs=(hbm, hbm),
        scratch_shapes=[pltpu.SemaphoreType.DMA((2,))],
        compiler_params=pltpu.CompilerParams(vmem_limit_bytes=1024 * 1024),
        name="keep_results",
    )(*results))


def fits_fused(mesh, args):
    groups, blocks = mesh.shape["group"], mesh.shape["blk"]
    rows = args[6].shape[0] // (groups * blocks)
    steps = args[2].shape[0]
    return rows % 16 == 0 and blocks % 4 == 0 and blocks > 4 and groups > 1 and steps > 1


def solution(mesh):
    in_specs = (
        P(("group", "blk"), None),
        P(("group", "blk"), None),
        P(None, ("group", "blk"), None),
        P(),
        P(),
        P(),
        P(("group", "blk"), None),
        P(("group", "blk"), None),
    )
    out_specs = (P(("group", "blk"), None), P(("group", "blk"), None))
    def run(*args):
        body = on_device_fused if fits_fused(mesh, args) else on_device
        return jax.shard_map(
            body, mesh=mesh, in_specs=in_specs, out_specs=out_specs, check_vma=False
        )(*args)

    return run
```

```python
import functools

import jax
import jax.numpy as jnp
from jax import lax
from jax.experimental import pallas as pl
from jax.experimental.pallas import tpu as pltpu
from jax.sharding import PartitionSpec as P

learn_rate = 0.2
tiny_floor = 1e-10
COLUMNS = 4
PAIR = 2
HALVES = 2
CUTS = (0, 1, 2)
PIECES = len(CUTS) - 1
PACE, HOP_Z, HOP_PLANE = 0.7, 3.4, 3.2


def schedule():
    chunks = COLUMNS * HALVES
    lot = PAIR * HALVES
    timed = [(-2.0 + k / lot / 2, i, "b", k) for i, k in enumerate(range(0, chunks, lot))]
    for k in range(chunks):
        at = k * PACE
        timed += [(-1.0, 1, "g", k), (at, 2, "r", k), (at + HOP_Z, 3, "u", k), (at + 2 * HOP_Z, 4, "G", k)]
        timed += [(at + 2 * HOP_Z + HOP_PLANE, 5, "C", k)]
    begun = sorted(t for t in timed if t[2] == "b")
    order = [t[2:] for t in begun] + [t[2:] for t in sorted(t for t in timed if t[2] != "b")]
    for k in range(0, chunks, lot):
        order.insert(order.index(("C", k + lot - 1)) + 1, ("n", k))
        ahead = ("C", min(k + lot + lot - 2, chunks - 1))
        order.insert(len(order) if k + lot == chunks else order.index(ahead) + 1, ("f", k))
    return order


SCHEDULE = schedule()


def from_behind(block, axis, distance):
    devices = range(lax.axis_size(axis))
    route = [((i - distance) % len(devices), i) for i in devices]
    return lax.ppermute(block, axis, route)


def contract_rows(left, right):
    return lax.dot_general(
        left, right, (((0,), (0,)), ((), ())), preferred_element_type=jnp.float32
    )


def contract_cols(left, right):
    return lax.dot_general(
        left, right, (((1,), (1,)), ((), ())), preferred_element_type=jnp.float32
    )


def unpack_bits(words):
    shifts = jnp.arange(8, dtype=jnp.int32)
    bits = jnp.bitwise_and(jnp.right_shift(words[:, :, None], shifts[None, None, :]), 1)
    return bits.reshape(words.shape[0], words.shape[1] * 8)


def step_gradient(head_block, tail_block, label_words, operator):
    projected = contract_cols(operator, tail_block).astype(jnp.bfloat16)
    scores = jnp.dot(head_block, projected, preferred_element_type=jnp.float32)
    targets = unpack_bits(label_words).astype(jnp.float32)
    residual = (jax.nn.sigmoid(scores) - targets).astype(jnp.bfloat16)
    partial_sum = contract_rows(head_block, residual).astype(jnp.bfloat16)
    return jnp.dot(partial_sum, tail_block, preferred_element_type=jnp.float32)


def on_device(head_rows, tail_rows, labels, relations, hot_ids, row_order, master, grad_squares):
    rel_count = relations.shape[0]
    model_width = relations.shape[1]
    step_count = labels.shape[0]
    gradient = jnp.zeros((rel_count, model_width, model_width), jnp.float32)
    tail_block = tail_rows
    for cycle_step in range(step_count):
        if cycle_step > 0:
            tail_block = from_behind(tail_block, "blk", 1)
        relation_id = hot_ids[cycle_step]
        step_term = step_gradient(head_rows, tail_block, labels[cycle_step], relations[relation_id])
        gradient = gradient.at[relation_id].add(step_term)
    table_rows = rel_count * model_width
    flat_gradient = gradient.reshape(table_rows, model_width)
    groups = lax.axis_size("group")
    blocks = lax.axis_size("blk")
    slot_rows = row_order.reshape(groups, blocks, -1).transpose(1, 0, 2).reshape(-1)
    first_sum = lax.psum_scatter(
        jnp.take(flat_gradient, slot_rows, axis=0), "blk", scatter_dimension=0, tiled=True
    )
    owned_sum = lax.psum_scatter(first_sum, "group", scatter_dimension=0, tiled=True)
    squares_new = grad_squares + owned_sum * owned_sum
    new_master = master - learn_rate * owned_sum / (jnp.sqrt(squares_new) + tiny_floor)
    updated = new_master.astype(jnp.bfloat16)
    group_rows = lax.all_gather(updated, "group", axis=0, tiled=True)
    gathered = lax.all_gather(group_rows, "blk", axis=0, tiled=True)
    positions = (
        jnp.zeros((table_rows,), jnp.int32)
        .at[slot_rows]
        .set(jnp.arange(table_rows, dtype=jnp.int32))
    )
    chosen = lax.dynamic_slice_in_dim(
        positions, hot_ids[step_count - 1] * model_width, model_width, 0
    )
    operator = jnp.take(gathered, chosen, axis=0)
    transformed = jnp.dot(head_rows, operator, preferred_element_type=jnp.float32).astype(
        jnp.bfloat16
    )
    return (new_master, transformed)


MESH = pl.DeviceIdType.MESH


def fused_body(
    dims, hot_src, order_src, head_src, tail_src, labels_src, relations_src, master_src, squares_src,
    new_master, transformed,
    hot, order, head, tail, labels, relations, master, squares, tails, head_t, pick, near_pick, far_pick,
    picked, targets, scaled, partials, last_partial, gradient, stored_early, near_part, own, core_in, pair_sum, group_in,
    group_sum, rest_in, table, send_sems, recv_sems, tail_send, tail_recv, load_sems,
):
    groups, deep, rows, columns, width = dims
    chunks = columns * HALVES
    part = rows // HALVES
    blocks = 4 * deep
    plane = 2 * groups
    step_count, model_width = labels.shape[0], head.shape[1]
    rel_count = relations.shape[0]
    total_rows = order.shape[1]
    g = lax.axis_index("group")
    b = lax.axis_index("blk")
    core = lax.rem(b, 2)
    mid = lax.rem(b // 2, 2)
    z = b // 4
    spot = g * 2 + mid
    partner = (g, b + 1 - 2 * core)
    plane_spots = [lax.rem(spot + d, plane) for d in range(1, plane)]
    group_peers = [(p // 2, z * 4 + lax.rem(p, 2) * 2 + core) for p in plane_spots]
    rest_peers = [(g, lax.rem(z + d, deep) * 4 + mid * 2 + core) for d in range(1, deep)]
    right = (g, lax.rem(b + 1, blocks))
    left = (g, lax.rem(b + blocks - 1, blocks))

    barrier = pltpu.get_barrier_semaphore()
    greeted = [partner] + group_peers + rest_peers + [right, left]
    for peer in greeted:
        pl.semaphore_signal(barrier, inc=1, device_id=peer, device_id_type=MESH)

    sources = (hot_src, head_src, relations_src, tail_src, labels_src, order_src, master_src, squares_src)
    filled = (hot, head, relations, tail, labels, order, master, squares)
    loads = [
        pltpu.make_async_copy(source, target, load_sems.at[i])
        for i, (source, target) in enumerate(zip(sources, filled))
    ]
    for load in loads:
        load.start()
    pl.semaphore_wait(barrier, len(greeted))

    def send(source, target, index, peer):
        copy = pltpu.make_async_remote_copy(
            src_ref=source, dst_ref=target, send_sem=send_sems.at[index],
            recv_sem=recv_sems.at[index], device_id=peer, device_id_type=MESH,
        )
        copy.start()
        return copy

    class Lot:
        def __init__(self, index, copies, like):
            for source, target, peer in copies:
                send(source, target, index, peer)
            self.index, self.like = index, like

        def wait_recv(self):
            pltpu.make_async_copy(self.like, self.like, recv_sems.at[self.index]).wait()

        def wait_send(self):
            pltpu.make_async_copy(self.like, self.like, send_sems.at[self.index]).wait()

    tail_count = tail.shape[0]
    piece = tail_count // CUTS[-1]
    pieces = [slice(start * piece, end * piece) for start, end in zip(CUTS, CUTS[1:])]

    def send_tail(step, p):
        source = tail_src if step == 0 else tails.at[step - 1]
        copy = pltpu.make_async_remote_copy(
            src_ref=source.at[pieces[p]], dst_ref=tails.at[step, pieces[p]],
            send_sem=tail_send.at[step, p], recv_sem=tail_recv.at[step, p],
            device_id=right, device_id_type=MESH,
        )
        copy.start()
        return copy

    def tail_of(step):
        return tail if step == 0 else tails.at[step - 1]

    f32, bf16 = jnp.float32, jnp.bfloat16
    word_count = labels.shape[1]
    last = step_count - 1
    hops = {(0, p): send_tail(0, p) for p in range(PIECES)}

    def arrive(step, p):
        hops[step - 1, p].wait_recv()
        if step < last:
            hops[step, p] = send_tail(step, p)

    def step_targets(step):
        lane = lax.broadcasted_iota(jnp.int32, (word_count, tail_count), 1)
        word = lax.broadcasted_iota(jnp.int32, (word_count, tail_count), 0)
        spread = (lane // 8 == word).astype(f32).astype(bf16)
        words = contract_rows(labels[step].astype(f32).astype(bf16), spread).astype(jnp.int32)
        bit = lax.broadcasted_iota(jnp.int32, words.shape, 1) % 8
        targets[step] = ((words >> bit) & 1).astype(f32).astype(bf16)

    def step_scaled(step):
        scaled[step] = jnp.dot(head[...], relations[hot[step]], preferred_element_type=f32).astype(bf16)

    def step_partial(step, span, heads):
        scores = contract_cols(scaled[step], tail_of(step)[span])
        residual = (jax.nn.sigmoid(scores) - targets[step, :, span].astype(f32)).astype(bf16)
        return jnp.dot(heads, residual, preferred_element_type=f32).astype(bf16)

    def add_term(step):
        term = jnp.dot(partials[step], tail_of(step)[...], preferred_element_type=f32)
        for r in range(rel_count):
            share = (hot[step] == r).astype(f32) * term
            gradient[r] = share if step == 0 else gradient[r] + share

    def pick_rows():
        spread_order = jnp.broadcast_to(order[...].astype(f32), (128, total_rows)).T
        for j in range(0, total_rows, 128):
            ids = lax.broadcasted_iota(jnp.int32, (total_rows, 128), 1).astype(f32) + j
            pick[:, j : j + 128] = (spread_order == ids).astype(f32).astype(bf16)
        first = (hot[last] * model_width).astype(f32)
        chosen = jnp.concatenate([
            (spread_order - first == lax.broadcasted_iota(jnp.int32, (total_rows, 128), 1).astype(f32) + j)
            .astype(f32).astype(bf16)
            for j in range(0, model_width, 128)
        ], axis=1)
        picked[...] = jnp.dot(chosen, head_t[...], preferred_element_type=f32).astype(bf16).reshape(picked.shape)
        half = total_rows // 2
        near_pick[...] = picked[:, core].reshape(half, head.shape[0]).T
        far_pick[...] = picked[:, 1 - core].reshape(half, head.shape[0]).T

    for load in loads:
        load.wait()
    with jax.named_scope("s0"):
        head_t[...] = head[...].T
        step_targets(0)
        step_scaled(0)
        partials[0] = step_partial(0, slice(0, tail_count), head_t[...])
        add_term(0)
    with jax.named_scope("t12"):
        for step in range(1, step_count):
            step_targets(step)
            step_scaled(step)
    with jax.named_scope("a10"):
        if last > 1:
            arrive(1, 0)
    with jax.named_scope("pick"):
        pick_rows()
    for step in range(1, last):
        for p in range(PIECES):
            if step > 1 or p > 0:
                with jax.named_scope(f"a{step}{p}"):
                    arrive(step, p)
            with jax.named_scope(f"p{step}{p}"):
                partials[step, :, pieces[p]] = step_partial(step, pieces[p], head_t[...])
        with jax.named_scope(f"add{step}"):
            add_term(step)
    with jax.named_scope("stored"):
        stored_early[...] = jnp.dot(
            pick[...], gradient[...].reshape(total_rows, model_width).astype(bf16), preferred_element_type=f32
        )
    for p in range(PIECES):
        with jax.named_scope(f"a{last}{p}"):
            arrive(last, p)
        with jax.named_scope(f"p{last}{p}"):
            last_partial[:, pieces[p]] = step_partial(last, pieces[p], picked[...].reshape(total_rows, head.shape[0]))

    core_copies = [None] * chunks
    group_copies = [None] * chunks
    rest_copies = [None] * chunks
    back_rest = [None] * chunks
    back_group = [None] * chunks
    back_core = [None] * chunks

    def place(k):
        column, half = k // HALVES, k % HALVES
        return column, slice(half * part, (half + 1) * part), slice(column * width, (column + 1) * width)

    def begin(k):
        first = k // HALVES
        cols = slice(first * width, (first + PAIR) * width)
        term = jnp.dot(last_partial[...], tail_of(last)[:, cols], preferred_element_type=f32)
        stored = (stored_early[:, cols] + term).astype(bf16).reshape(groups, deep, 2, 2, rows, PAIR * width)
        for i in range(k, k + PAIR * HALVES):
            column, lines, _ = place(i)
            own[i] = stored[:, :, :, :, lines, (column - first) * width : (column - first + 1) * width]
            core_copies[i] = [send(own.at[i, :, :, :, 1 - core], core_in.at[i], (i, 0), partner)]

    def over_group(k):
        for copy in core_copies[k]:
            copy.wait_recv()
        pair_sum[k] = (own[k, :, :, :, core].astype(f32) + core_in[k].astype(f32)).astype(bf16)
        group_copies[k] = [Lot((k, 1), [
            (pair_sum.at[k, p // 2, :, lax.rem(p, 2)], group_in.at[k, d], peer)
            for d, (p, peer) in enumerate(zip(plane_spots, group_peers))
        ], group_in.at[k])]

    def over_rest(k):
        for copy in group_copies[k]:
            copy.wait_recv()
        summed = own[k, g, :, mid, core].astype(f32) + core_in[k, g, :, mid].astype(f32)
        for d in range(plane - 1):
            summed = summed + group_in[k, d].astype(f32)
        group_sum[k] = summed.astype(bf16)
        rest_copies[k] = [Lot((k, 2), [
            (group_sum.at[k, lax.rem(z + d + 1, deep)], rest_in.at[k, d], peer)
            for d, peer in enumerate(rest_peers)
        ], rest_in.at[k])]

    def update(k):
        column, lines, cols = place(k)
        for copy in rest_copies[k]:
            copy.wait_recv()
        summed = group_sum[k, z].astype(f32)
        for d in range(deep - 1):
            summed = summed + rest_in[k, d].astype(f32)
        squares_new = squares[lines, cols] + summed * summed
        updated = master[lines, cols] - learn_rate * summed / (jnp.sqrt(squares_new) + tiny_floor)
        new_master[lines, cols] = updated
        table[column, g, z, mid, core, lines] = updated.astype(bf16)
        mine = table.at[column, g, z, mid, core, lines]
        back_rest[k] = [Lot((k, 3), [(mine, mine, peer) for peer in rest_peers], rest_in.at[k])]

    def drain(copies):
        for copy in copies:
            copy.wait_send()

    def gather_group(k):
        column, lines, _ = place(k)
        drain(core_copies[k] + group_copies[k])
        for copy in back_rest[k]:
            copy.wait_recv()
        mine = table.at[column, g, :, mid, core, lines]
        back_group[k] = [Lot((k, 4), [(mine, mine, peer) for peer in group_peers], group_in.at[k])]

    def gather_core(k):
        column, lines, _ = place(k)
        drain(rest_copies[k] + back_rest[k])
        if k == 0:
            drain(hops.values())
        if k > 1:
            drain(back_group[k - 2] + back_core[k - 2])
        for copy in back_group[k]:
            copy.wait_recv()
        mine = table.at[column, :, :, :, core, lines]
        back_core[k] = [send(mine, mine, (k, 5), partner)]

    def operator_of(k, side):
        first = k // HALVES
        return jnp.concatenate(
            [table[i, :, :, :, side].reshape(total_rows // 2, width) for i in range(first, first + PAIR)], axis=1
        )

    def near(k):
        near_part[k // (PAIR * HALVES)] = jnp.dot(near_pick[...], operator_of(k, core), preferred_element_type=f32)

    def finish(k):
        first = k // HALVES
        cols = slice(first * width, (first + PAIR) * width)
        if k + PAIR * HALVES == chunks:
            for i in range(max(chunks - 2, 0), chunks):
                drain(back_group[i])
        for i in range(k, k + PAIR * HALVES):
            for copy in back_core[i]:
                copy.wait_recv()
        far = jnp.dot(far_pick[...], operator_of(k, 1 - core), preferred_element_type=f32)
        transformed[:, cols] = (near_part[k // (PAIR * HALVES)] + far).astype(bf16)

    stages = dict(
        b=begin, g=over_group, r=over_rest, u=update, G=gather_group, C=gather_core, n=near, f=finish
    )
    for stage, k in SCHEDULE:
        with jax.named_scope(f"{stage}{k}"):
            stages[stage](k)

    for k in range(max(chunks - 2, 0), chunks):
        drain(back_core[k])


def on_device_fused(head_rows, tail_rows, labels, relations, hot_ids, row_order, master, grad_squares):
    groups = lax.axis_size("group")
    deep = lax.axis_size("blk") // 4
    rows, model_width = master.shape
    steps = labels.shape[0]
    heads = head_rows.shape[0]
    table_rows = relations.shape[0] * model_width
    columns = COLUMNS
    chunks = columns * HALVES
    part = rows // HALVES
    width = model_width // columns
    order = row_order.reshape(1, -1)
    copies = 6
    bf16 = jnp.bfloat16
    vmem = pl.BlockSpec(memory_space=pltpu.VMEM)
    hbm = pl.BlockSpec(memory_space=pltpu.HBM)
    words = labels.transpose(0, 2, 1)
    results = pl.pallas_call(
        functools.partial(fused_body, (groups, deep, rows, columns, width)),
        out_shape=(
            pltpu.VMEM(master.shape, jnp.float32),
            pltpu.VMEM((heads, model_width), bf16),
        ),
        in_specs=[hbm] * 8,
        out_specs=(vmem, vmem),
        scratch_shapes=[pltpu.SMEM(hot_ids.shape, hot_ids.dtype), pltpu.VMEM(order.shape, order.dtype)] + [
            pltpu.VMEM(x.shape, x.dtype)
            for x in (head_rows, tail_rows, words, relations, master, grad_squares)
        ] + [
            pltpu.VMEM((steps - 1,) + tail_rows.shape, bf16),
            pltpu.VMEM((model_width, heads), bf16),
            pltpu.VMEM((table_rows, table_rows), bf16),
            pltpu.VMEM((heads, table_rows // 2), bf16),
            pltpu.VMEM((heads, table_rows // 2), bf16),
            pltpu.VMEM((groups * deep * 2, 2, rows, heads), bf16),
            pltpu.VMEM((steps, heads, tail_rows.shape[0]), bf16),
            pltpu.VMEM((steps, heads, model_width), bf16),
            pltpu.VMEM((steps - 1, model_width, tail_rows.shape[0]), bf16),
            pltpu.VMEM((table_rows, tail_rows.shape[0]), bf16),
            pltpu.VMEM(relations.shape, jnp.float32),
            pltpu.VMEM((table_rows, model_width), jnp.float32),
            pltpu.VMEM((columns // PAIR, heads, PAIR * width), jnp.float32),
            pltpu.VMEM((chunks, groups, deep, 2, 2, part, width), bf16),
            pltpu.VMEM((chunks, groups, deep, 2, part, width), bf16),
            pltpu.VMEM((chunks, groups, deep, 2, part, width), bf16),
            pltpu.VMEM((chunks, 2 * groups - 1, deep, part, width), bf16),
            pltpu.VMEM((chunks, deep, part, width), bf16),
            pltpu.VMEM((chunks, deep - 1, part, width), bf16),
            pltpu.VMEM((columns, groups, deep, 2, 2, rows, width), bf16),
            pltpu.SemaphoreType.DMA((chunks, copies)),
            pltpu.SemaphoreType.DMA((chunks, copies)),
            pltpu.SemaphoreType.DMA((steps - 1, PIECES)),
            pltpu.SemaphoreType.DMA((steps - 1, PIECES)),
            pltpu.SemaphoreType.DMA((8,)),
        ],
        compiler_params=pltpu.CompilerParams(
            collective_id=0, has_side_effects=True, vmem_limit_bytes=60000 * 1024
        ),
        name="rescal_update",
    )(hot_ids, order, head_rows, tail_rows, words, relations, master, grad_squares)
    return keep_results(results)


def keep_body(first, second, first_out, second_out, sems):
    copies = [
        pltpu.make_async_copy(first, first_out, sems.at[0]),
        pltpu.make_async_copy(second, second_out, sems.at[1]),
    ]
    for copy in copies:
        copy.start()
    for copy in copies:
        copy.wait()


def keep_results(results):
    vmem = pl.BlockSpec(memory_space=pltpu.VMEM)
    hbm = pl.BlockSpec(memory_space=pltpu.HBM)
    return tuple(pl.pallas_call(
        keep_body,
        out_shape=tuple(jax.ShapeDtypeStruct(r.shape, r.dtype) for r in results),
        in_specs=[vmem, vmem],
        out_specs=(hbm, hbm),
        scratch_shapes=[pltpu.SemaphoreType.DMA((2,))],
        compiler_params=pltpu.CompilerParams(vmem_limit_bytes=1024 * 1024),
        name="keep_results",
    )(*results))


def fits_fused(mesh, args):
    groups, blocks = mesh.shape["group"], mesh.shape["blk"]
    rows = args[6].shape[0] // (groups * blocks)
    steps = args[2].shape[0]
    return rows % (16 * HALVES) == 0 and blocks % 4 == 0 and blocks > 4 and groups > 1 and steps > 1


def solution(mesh):
    in_specs = (
        P(("group", "blk"), None),
        P(("group", "blk"), None),
        P(None, ("group", "blk"), None),
        P(),
        P(),
        P(),
        P(("group", "blk"), None),
        P(("group", "blk"), None),
    )
    out_specs = (P(("group", "blk"), None), P(("group", "blk"), None))
    def run(*args):
        body = on_device_fused if fits_fused(mesh, args) else on_device
        return jax.shard_map(
            body, mesh=mesh, in_specs=in_specs, out_specs=out_specs, check_vma=False
        )(*args)

    return run
```

```python
import functools

import jax
import jax.numpy as jnp
from jax import lax
from jax.experimental import pallas as pl
from jax.experimental.pallas import tpu as pltpu
from jax.sharding import PartitionSpec as P

learn_rate = 0.2
tiny_floor = 1e-10
COLUMNS = 4
PAIR = 2
HALVES = 2
CUTS = (0, 1, 2)
PIECES = len(CUTS) - 1
PACE, HOP_Z, HOP_PLANE = 0.7, 3.4, 3.2


def schedule():
    chunks = COLUMNS * HALVES
    lot = PAIR * HALVES
    timed = [(-2.0 + k / lot / 2, i, "b", k) for i, k in enumerate(range(0, chunks, lot))]
    for k in range(chunks):
        at = k * PACE
        timed += [(-1.0, 1, "g", k), (at, 2, "r", k), (at + HOP_Z, 3, "u", k), (at + 2 * HOP_Z, 4, "G", k)]
        timed += [(at + 2 * HOP_Z + HOP_PLANE, 5, "C", k)]
    begun = sorted(t for t in timed if t[2] == "b")
    order = [t[2:] for t in begun] + [t[2:] for t in sorted(t for t in timed if t[2] != "b")]
    for k in range(0, chunks, lot):
        order.insert(order.index(("C", k + lot - 1)) + 1, ("n", k))
        ahead = ("C", min(k + lot + lot - 2, chunks - 1))
        order.insert(len(order) if k + lot == chunks else order.index(ahead) + 1, ("f", k))
    return order


SCHEDULE = schedule()


def from_behind(block, axis, distance):
    devices = range(lax.axis_size(axis))
    route = [((i - distance) % len(devices), i) for i in devices]
    return lax.ppermute(block, axis, route)


def contract_rows(left, right):
    return lax.dot_general(
        left, right, (((0,), (0,)), ((), ())), preferred_element_type=jnp.float32
    )


def contract_cols(left, right):
    return lax.dot_general(
        left, right, (((1,), (1,)), ((), ())), preferred_element_type=jnp.float32
    )


def unpack_bits(words):
    shifts = jnp.arange(8, dtype=jnp.int32)
    bits = jnp.bitwise_and(jnp.right_shift(words[:, :, None], shifts[None, None, :]), 1)
    return bits.reshape(words.shape[0], words.shape[1] * 8)


def step_gradient(head_block, tail_block, label_words, operator):
    projected = contract_cols(operator, tail_block).astype(jnp.bfloat16)
    scores = jnp.dot(head_block, projected, preferred_element_type=jnp.float32)
    targets = unpack_bits(label_words).astype(jnp.float32)
    residual = (jax.nn.sigmoid(scores) - targets).astype(jnp.bfloat16)
    partial_sum = contract_rows(head_block, residual).astype(jnp.bfloat16)
    return jnp.dot(partial_sum, tail_block, preferred_element_type=jnp.float32)


def on_device(head_rows, tail_rows, labels, relations, hot_ids, row_order, master, grad_squares):
    rel_count = relations.shape[0]
    model_width = relations.shape[1]
    step_count = labels.shape[0]
    gradient = jnp.zeros((rel_count, model_width, model_width), jnp.float32)
    tail_block = tail_rows
    for cycle_step in range(step_count):
        if cycle_step > 0:
            tail_block = from_behind(tail_block, "blk", 1)
        relation_id = hot_ids[cycle_step]
        step_term = step_gradient(head_rows, tail_block, labels[cycle_step], relations[relation_id])
        gradient = gradient.at[relation_id].add(step_term)
    table_rows = rel_count * model_width
    flat_gradient = gradient.reshape(table_rows, model_width)
    groups = lax.axis_size("group")
    blocks = lax.axis_size("blk")
    slot_rows = row_order.reshape(groups, blocks, -1).transpose(1, 0, 2).reshape(-1)
    first_sum = lax.psum_scatter(
        jnp.take(flat_gradient, slot_rows, axis=0), "blk", scatter_dimension=0, tiled=True
    )
    owned_sum = lax.psum_scatter(first_sum, "group", scatter_dimension=0, tiled=True)
    squares_new = grad_squares + owned_sum * owned_sum
    new_master = master - learn_rate * owned_sum / (jnp.sqrt(squares_new) + tiny_floor)
    updated = new_master.astype(jnp.bfloat16)
    group_rows = lax.all_gather(updated, "group", axis=0, tiled=True)
    gathered = lax.all_gather(group_rows, "blk", axis=0, tiled=True)
    positions = (
        jnp.zeros((table_rows,), jnp.int32)
        .at[slot_rows]
        .set(jnp.arange(table_rows, dtype=jnp.int32))
    )
    chosen = lax.dynamic_slice_in_dim(
        positions, hot_ids[step_count - 1] * model_width, model_width, 0
    )
    operator = jnp.take(gathered, chosen, axis=0)
    transformed = jnp.dot(head_rows, operator, preferred_element_type=jnp.float32).astype(
        jnp.bfloat16
    )
    return (new_master, transformed)


MESH = pl.DeviceIdType.MESH


def fused_body(
    dims, hot_src, order_src, head_src, tail_src, labels_src, relations_src, master_src, squares_src,
    new_master, transformed,
    hot, order, head, tail, labels, relations, master, squares, tails, head_t, pick, near_pick, far_pick,
    picked, targets, scaled, partials, last_partial, gradient, stored_early, near_part, own, core_in, pair_sum, group_in,
    group_sum, rest_in, table, send_sems, recv_sems, tail_send, tail_recv, load_sems,
):
    groups, deep, rows, columns, width = dims
    chunks = columns * HALVES
    part = rows // HALVES
    blocks = 4 * deep
    plane = 2 * groups
    step_count, model_width = labels.shape[0], head.shape[1]
    rel_count = relations.shape[0]
    total_rows = order.shape[1]
    g = lax.axis_index("group")
    b = lax.axis_index("blk")
    core = lax.rem(b, 2)
    mid = lax.rem(b // 2, 2)
    z = b // 4
    spot = g * 2 + mid
    partner = (g, b + 1 - 2 * core)
    plane_spots = [lax.rem(spot + d, plane) for d in range(1, plane)]
    group_peers = [(p // 2, z * 4 + lax.rem(p, 2) * 2 + core) for p in plane_spots]
    rest_peers = [(g, lax.rem(z + d, deep) * 4 + mid * 2 + core) for d in range(1, deep)]
    right = (g, lax.rem(b + 1, blocks))
    left = (g, lax.rem(b + blocks - 1, blocks))

    barrier = pltpu.get_barrier_semaphore()
    greeted = [partner] + group_peers + rest_peers + [right, left]
    for peer in greeted:
        pl.semaphore_signal(barrier, inc=1, device_id=peer, device_id_type=MESH)

    sources = (hot_src, head_src, relations_src, tail_src, labels_src, order_src, master_src, squares_src)
    filled = (hot, head, relations, tail, labels, order, master, squares)
    loads = [
        pltpu.make_async_copy(source, target, load_sems.at[i])
        for i, (source, target) in enumerate(zip(sources, filled))
    ]
    for load in loads:
        load.start()
    pl.semaphore_wait(barrier, len(greeted))

    def send(source, target, index, peer):
        copy = pltpu.make_async_remote_copy(
            src_ref=source, dst_ref=target, send_sem=send_sems.at[index[1]],
            recv_sem=recv_sems.at[index], device_id=peer, device_id_type=MESH,
        )
        copy.start()
        return copy

    class Lot:
        def __init__(self, index, copies, like):
            for source, target, peer in copies:
                send(source, target, index, peer)
            self.index, self.like = index, like

        def wait_recv(self):
            pltpu.make_async_copy(self.like, self.like, recv_sems.at[self.index]).wait()

    tail_count = tail.shape[0]
    piece = tail_count // CUTS[-1]
    pieces = [slice(start * piece, end * piece) for start, end in zip(CUTS, CUTS[1:])]

    def send_tail(step, p):
        source = tail_src if step == 0 else tails.at[step - 1]
        copy = pltpu.make_async_remote_copy(
            src_ref=source.at[pieces[p]], dst_ref=tails.at[step, pieces[p]],
            send_sem=tail_send.at[step, p], recv_sem=tail_recv.at[step, p],
            device_id=right, device_id_type=MESH,
        )
        copy.start()
        return copy

    def tail_of(step):
        return tail if step == 0 else tails.at[step - 1]

    f32, bf16 = jnp.float32, jnp.bfloat16
    word_count = labels.shape[1]
    last = step_count - 1
    hops = {(0, p): send_tail(0, p) for p in range(PIECES)}

    def arrive(step, p):
        hops[step - 1, p].wait_recv()
        if step < last:
            hops[step, p] = send_tail(step, p)

    def step_targets(step):
        lane = lax.broadcasted_iota(jnp.int32, (word_count, tail_count), 1)
        word = lax.broadcasted_iota(jnp.int32, (word_count, tail_count), 0)
        spread = (lane // 8 == word).astype(f32).astype(bf16)
        words = contract_rows(labels[step].astype(f32).astype(bf16), spread).astype(jnp.int32)
        bit = lax.broadcasted_iota(jnp.int32, words.shape, 1) % 8
        targets[step] = (0.5 - ((words >> bit) & 1).astype(f32)).astype(bf16)

    def step_scaled(step):
        scaled[step] = jnp.dot(head[...], relations[hot[step]], preferred_element_type=f32).astype(bf16)

    def step_partial(step, span, heads):
        scores = contract_cols(scaled[step], tail_of(step)[span])
        residual = (0.5 * jnp.tanh(0.5 * scores) + targets[step, :, span].astype(f32)).astype(bf16)
        return jnp.dot(heads, residual, preferred_element_type=f32).astype(bf16)

    def add_term(step):
        term = jnp.dot(partials[step], tail_of(step)[...], preferred_element_type=f32)
        for r in range(rel_count):
            share = (hot[step] == r).astype(f32) * term
            gradient[r] = share if step == 0 else gradient[r] + share

    def pick_rows():
        spread_order = jnp.broadcast_to(order[...].astype(f32), (128, total_rows)).T
        for j in range(0, total_rows, 128):
            ids = lax.broadcasted_iota(jnp.int32, (total_rows, 128), 1).astype(f32) + j
            pick[:, j : j + 128] = (spread_order == ids).astype(f32).astype(bf16)
        first = (hot[last] * model_width).astype(f32)
        chosen = jnp.concatenate([
            (spread_order - first == lax.broadcasted_iota(jnp.int32, (total_rows, 128), 1).astype(f32) + j)
            .astype(f32).astype(bf16)
            for j in range(0, model_width, 128)
        ], axis=1)
        picked[...] = jnp.dot(chosen, head_t[...], preferred_element_type=f32).astype(bf16).reshape(picked.shape)
        half = total_rows // 2
        near_pick[...] = picked[:, core].reshape(half, head.shape[0]).T
        far_pick[...] = picked[:, 1 - core].reshape(half, head.shape[0]).T

    for load in loads:
        load.wait()
    with jax.named_scope("s0"):
        head_t[...] = head[...].T
        step_targets(0)
        step_scaled(0)
        partials[0] = step_partial(0, slice(0, tail_count), head_t[...])
        add_term(0)
    with jax.named_scope("t12"):
        for step in range(1, step_count):
            step_targets(step)
            step_scaled(step)
    with jax.named_scope("a10"):
        if last > 1:
            arrive(1, 0)
    with jax.named_scope("pick"):
        pick_rows()
    for step in range(1, last):
        for p in range(PIECES):
            if step > 1 or p > 0:
                with jax.named_scope(f"a{step}{p}"):
                    arrive(step, p)
            with jax.named_scope(f"p{step}{p}"):
                partials[step, :, pieces[p]] = step_partial(step, pieces[p], head_t[...])
        with jax.named_scope(f"add{step}"):
            add_term(step)
    with jax.named_scope("stored"):
        stored_early[...] = jnp.dot(
            pick[...], gradient[...].reshape(total_rows, model_width).astype(bf16), preferred_element_type=f32
        )
    for p in range(PIECES):
        with jax.named_scope(f"a{last}{p}"):
            arrive(last, p)
        with jax.named_scope(f"p{last}{p}"):
            last_partial[:, pieces[p]] = step_partial(last, pieces[p], picked[...].reshape(total_rows, head.shape[0]))
            if p < PIECES - 1:
                stored_early[...] += jnp.dot(
                    last_partial[:, pieces[p]], tail_of(last)[pieces[p]], preferred_element_type=f32
                )

    core_copies = [None] * chunks
    group_copies = [None] * chunks
    rest_copies = [None] * chunks
    back_rest = [None] * chunks
    back_group = [None] * chunks
    back_core = [None] * chunks

    def place(k):
        column, half = k // HALVES, k % HALVES
        return column, slice(half * part, (half + 1) * part), slice(column * width, (column + 1) * width)

    def begin(k):
        first = k // HALVES
        cols = slice(first * width, (first + PAIR) * width)
        term = jnp.dot(last_partial[:, pieces[-1]], tail_of(last)[pieces[-1], cols], preferred_element_type=f32)
        stored = (stored_early[:, cols] + term).astype(bf16).reshape(groups, deep, 2, 2, rows, PAIR * width)
        for i in range(k, k + PAIR * HALVES):
            column, lines, _ = place(i)
            own[i] = stored[:, :, :, :, lines, (column - first) * width : (column - first + 1) * width]
            core_copies[i] = [send(own.at[i, :, :, :, 1 - core], core_in.at[i], (i, 0), partner)]

    def over_group(k):
        for copy in core_copies[k]:
            copy.wait_recv()
        pair_sum[k] = (own[k, :, :, :, core].astype(f32) + core_in[k].astype(f32)).astype(bf16)
        group_copies[k] = [Lot((k, 1), [
            (pair_sum.at[k, p // 2, :, lax.rem(p, 2)], group_in.at[k, d], peer)
            for d, (p, peer) in enumerate(zip(plane_spots, group_peers))
        ], group_in.at[k])]

    def over_rest(k):
        for copy in group_copies[k]:
            copy.wait_recv()
        summed = own[k, g, :, mid, core].astype(f32) + core_in[k, g, :, mid].astype(f32)
        for d in range(plane - 1):
            summed = summed + group_in[k, d].astype(f32)
        group_sum[k] = summed.astype(bf16)
        rest_copies[k] = [Lot((k, 2), [
            (group_sum.at[k, lax.rem(z + d + 1, deep)], rest_in.at[k, d], peer)
            for d, peer in enumerate(rest_peers)
        ], rest_in.at[k])]

    def update(k):
        column, lines, cols = place(k)
        for copy in rest_copies[k]:
            copy.wait_recv()
        summed = group_sum[k, z].astype(f32)
        for d in range(deep - 1):
            summed = summed + rest_in[k, d].astype(f32)
        squares_new = squares[lines, cols] + summed * summed
        updated = master[lines, cols] - learn_rate * summed / (jnp.sqrt(squares_new) + tiny_floor)
        new_master[lines, cols] = updated
        table[column, g, z, mid, core, lines] = updated.astype(bf16)
        mine = table.at[column, g, z, mid, core, lines]
        back_rest[k] = [Lot((k, 3), [(mine, mine, peer) for peer in rest_peers], rest_in.at[k])]

    def drain(copies):
        for copy in copies:
            copy.wait_send()

    def gather_group(k):
        column, lines, _ = place(k)
        for copy in back_rest[k]:
            copy.wait_recv()
        mine = table.at[column, g, :, mid, core, lines]
        back_group[k] = [Lot((k, 4), [(mine, mine, peer) for peer in group_peers], group_in.at[k])]

    def gather_core(k):
        column, lines, _ = place(k)
        if k == 0:
            drain(hops.values())
        for copy in back_group[k]:
            copy.wait_recv()
        mine = table.at[column, :, :, :, core, lines]
        back_core[k] = [send(mine, mine, (k, 5), partner)]

    def operator_of(k, side):
        first = k // HALVES
        return jnp.concatenate(
            [table[i, :, :, :, side].reshape(total_rows // 2, width) for i in range(first, first + PAIR)], axis=1
        )

    def near(k):
        near_part[k // (PAIR * HALVES)] = jnp.dot(near_pick[...], operator_of(k, core), preferred_element_type=f32)

    def finish(k):
        first = k // HALVES
        cols = slice(first * width, (first + PAIR) * width)
        if k + PAIR * HALVES == chunks:
            for i, like in enumerate((core_in, group_in, rest_in, rest_in)):
                pltpu.make_async_copy(like, like, send_sems.at[i]).wait()
        for i in range(k, k + PAIR * HALVES):
            for copy in back_core[i]:
                copy.wait_recv()
        far = jnp.dot(far_pick[...], operator_of(k, 1 - core), preferred_element_type=f32)
        transformed[:, cols] = (near_part[k // (PAIR * HALVES)] + far).astype(bf16)

    stages = dict(
        b=begin, g=over_group, r=over_rest, u=update, G=gather_group, C=gather_core, n=near, f=finish
    )
    for stage, k in SCHEDULE:
        with jax.named_scope(f"{stage}{k}"):
            stages[stage](k)

    for i, like in ((4, group_in), (5, core_in)):
        pltpu.make_async_copy(like, like, send_sems.at[i]).wait()


def on_device_fused(head_rows, tail_rows, labels, relations, hot_ids, row_order, master, grad_squares):
    groups = lax.axis_size("group")
    deep = lax.axis_size("blk") // 4
    rows, model_width = master.shape
    steps = labels.shape[0]
    heads = head_rows.shape[0]
    table_rows = relations.shape[0] * model_width
    columns = COLUMNS
    chunks = columns * HALVES
    part = rows // HALVES
    width = model_width // columns
    order = row_order.reshape(1, -1)
    copies = 6
    bf16 = jnp.bfloat16
    vmem = pl.BlockSpec(memory_space=pltpu.VMEM)
    hbm = pl.BlockSpec(memory_space=pltpu.HBM)
    words = labels.transpose(0, 2, 1)
    results = pl.pallas_call(
        functools.partial(fused_body, (groups, deep, rows, columns, width)),
        out_shape=(
            pltpu.VMEM(master.shape, jnp.float32),
            pltpu.VMEM((heads, model_width), bf16),
        ),
        in_specs=[hbm] * 8,
        out_specs=(vmem, vmem),
        scratch_shapes=[pltpu.SMEM(hot_ids.shape, hot_ids.dtype), pltpu.VMEM(order.shape, order.dtype)] + [
            pltpu.VMEM(x.shape, x.dtype)
            for x in (head_rows, tail_rows, words, relations, master, grad_squares)
        ] + [
            pltpu.VMEM((steps - 1,) + tail_rows.shape, bf16),
            pltpu.VMEM((model_width, heads), bf16),
            pltpu.VMEM((table_rows, table_rows), bf16),
            pltpu.VMEM((heads, table_rows // 2), bf16),
            pltpu.VMEM((heads, table_rows // 2), bf16),
            pltpu.VMEM((groups * deep * 2, 2, rows, heads), bf16),
            pltpu.VMEM((steps, heads, tail_rows.shape[0]), bf16),
            pltpu.VMEM((steps, heads, model_width), bf16),
            pltpu.VMEM((steps - 1, model_width, tail_rows.shape[0]), bf16),
            pltpu.VMEM((table_rows, tail_rows.shape[0]), bf16),
            pltpu.VMEM(relations.shape, jnp.float32),
            pltpu.VMEM((table_rows, model_width), jnp.float32),
            pltpu.VMEM((columns // PAIR, heads, PAIR * width), jnp.float32),
            pltpu.VMEM((chunks, groups, deep, 2, 2, part, width), bf16),
            pltpu.VMEM((chunks, groups, deep, 2, part, width), bf16),
            pltpu.VMEM((chunks, groups, deep, 2, part, width), bf16),
            pltpu.VMEM((chunks, 2 * groups - 1, deep, part, width), bf16),
            pltpu.VMEM((chunks, deep, part, width), bf16),
            pltpu.VMEM((chunks, deep - 1, part, width), bf16),
            pltpu.VMEM((columns, groups, deep, 2, 2, rows, width), bf16),
            pltpu.SemaphoreType.DMA((copies,)),
            pltpu.SemaphoreType.DMA((chunks, copies)),
            pltpu.SemaphoreType.DMA((steps - 1, PIECES)),
            pltpu.SemaphoreType.DMA((steps - 1, PIECES)),
            pltpu.SemaphoreType.DMA((8,)),
        ],
        compiler_params=pltpu.CompilerParams(
            collective_id=0, has_side_effects=True, vmem_limit_bytes=60000 * 1024
        ),
        name="rescal_update",
    )(hot_ids, order, head_rows, tail_rows, words, relations, master, grad_squares)
    return keep_results(results)


def keep_body(first, second, first_out, second_out, sems):
    copies = [
        pltpu.make_async_copy(first, first_out, sems.at[0]),
        pltpu.make_async_copy(second, second_out, sems.at[1]),
    ]
    for copy in copies:
        copy.start()
    for copy in copies:
        copy.wait()


def keep_results(results):
    vmem = pl.BlockSpec(memory_space=pltpu.VMEM)
    hbm = pl.BlockSpec(memory_space=pltpu.HBM)
    return tuple(pl.pallas_call(
        keep_body,
        out_shape=tuple(jax.ShapeDtypeStruct(r.shape, r.dtype) for r in results),
        in_specs=[vmem, vmem],
        out_specs=(hbm, hbm),
        scratch_shapes=[pltpu.SemaphoreType.DMA((2,))],
        compiler_params=pltpu.CompilerParams(vmem_limit_bytes=1024 * 1024),
        name="keep_results",
    )(*results))


def fits_fused(mesh, args):
    groups, blocks = mesh.shape["group"], mesh.shape["blk"]
    rows = args[6].shape[0] // (groups * blocks)
    steps = args[2].shape[0]
    return rows % (16 * HALVES) == 0 and blocks % 4 == 0 and blocks > 4 and groups > 1 and steps > 1


def solution(mesh):
    in_specs = (
        P(("group", "blk"), None),
        P(("group", "blk"), None),
        P(None, ("group", "blk"), None),
        P(),
        P(),
        P(),
        P(("group", "blk"), None),
        P(("group", "blk"), None),
    )
    out_specs = (P(("group", "blk"), None), P(("group", "blk"), None))
    def run(*args):
        body = on_device_fused if fits_fused(mesh, args) else on_device
        return jax.shard_map(
            body, mesh=mesh, in_specs=in_specs, out_specs=out_specs, check_vma=False
        )(*args)

    return run
```
